32 devices in a mesh: groups: 2 (over x), mix: 16 (over z, y, core).
Axes of the slice: x: 2, y: 2, z: 4, core: 2. Of those that a mesh axis runs over, the one named last changes fastest.
Arguments:
- recording: bfloat16 [8, 16384, 768], P('groups', 'mix'), parts along dimension 0, may hold values from -6 to 6
- mix_gain: float32 [1, 768], replicated, may hold values from 0.25 to 1.75
- block_weights: bfloat16 [1, 4, 128, 2, 128, 128], P(None, None, 'mix'), may hold values from -0.375 to 0.375
- section_perm: int32 [1, 4, 128], replicated, may hold values from 0 to 127, each once within a row
- block_mask: int32 [1, 4, 128], P(None, None, 'mix'), may hold values 0 or 1
- ffn_gain: float32 [1, 768], replicated, may hold values from 0.25 to 1.75
- ffn_in: bfloat16 [1, 2, 768, 2048], P(None, None, None, 'mix'), may hold values from -0.21875 to 0.21875
- ffn_out: bfloat16 [1, 768, 2048], P(None, None, 'mix'), may hold values from -0.125 to 0.125
Outputs:
- encoded: bfloat16 [8, 16384, 768], P('groups', 'mix'), parts along dimension 0
The draws below stay inside these ranges and needn't reach their ends.
There are 2 independent parts, one for each index of `groups`. The reference program is written for one: setup_inputs(seed, part) draws one part's arguments, and reference() takes and returns one part's arrays. A program takes and returns all parts, laid end to end along the dimension named above; an argument that names none is the same for every part. Nothing has to cross between parts.
Inputs may be any that keep to these rules, and one draw needn't show every extreme that they name: Each row section_perm[l, s] holds every number of 0 to 127 once.
All inputs are finite; a program needn't handle non-finite values. No bound on the sum of `block_mask` on one device may be relied on, other than what follows from the above.
Results may differ from the reference program's by a relative error of at most 0.013.
Values may be sent and summed in bfloat16 or wider, within the bound.
A program may use at most 192 MiB of HBM per device.

```python
import jax
import jax.numpy as jnp
from jax import lax

CH = 16384
BLK = 128
NB = 128
D = 768
FF = 2048
SECTIONS = 4
LAYERS = 1
TT = 4


def set_ends(array, own_key, smallest, top_value):
    spot = [jax.random.randint(jax.random.fold_in(own_key, axis), (), 0, length) for axis, length in enumerate(array.shape)]
    main_axis = array.shape.index(max(array.shape))
    neighbour = spot[:main_axis] + [(spot[main_axis] + 1) % array.shape[main_axis]] + spot[main_axis + 1:]
    return array.at[tuple(spot)].set(smallest).at[tuple(neighbour)].set(top_value)


def levels(rng, dims, shards, smallest, largest):
    def one(dim, parts):
        steps = jax.random.uniform(jax.random.fold_in(jax.random.fold_in(rng, 6), dim), (parts,), jnp.float32, smallest / len(shards), largest / len(shards))
        return jnp.repeat(jnp.exp(steps), dims[dim] // parts).reshape((-1,) + (1,) * (len(dims) - dim - 1))

    factor_of = one(*shards[0])
    for cut in shards[1:]:
        factor_of = factor_of * one(*cut)
    return factor_of


def normal_values(stream_key, extent, deviation, most, cuts=(), held_as=jnp.bfloat16):
    factor_of = levels(stream_key, extent, cuts, -0.22, 0.18) if cuts else 1.0
    values = jax.random.normal(stream_key, extent, jnp.float32) * deviation * factor_of
    return jnp.minimum(jnp.maximum(values, -most), most).astype(held_as)


def setup_inputs(seed: int = 0, part: int = 0) -> dict:
    keys = jax.random.split(jax.random.key(seed), 9)
    part_splits = jax.random.split(jax.random.fold_in(keys[8], part), 9)
    recording = normal_values(part_splits[0], (TT, CH, D), 1.0, 6.0, ((1, 16),))
    mix_gain = jnp.clip(1.0 + 0.15 * jax.random.normal(keys[1], (LAYERS, D), jnp.float32), 0.25, 1.75)
    block_weights = normal_values(keys[2], (LAYERS, SECTIONS, NB, 2, BLK, BLK), (2 * BLK) ** -0.5, 0.375, ((2, 16),))
    section_perm = jax.vmap(lambda own: jax.random.permutation(own, BLK))(jax.random.split(keys[3], LAYERS * SECTIONS)).reshape((LAYERS, SECTIONS, BLK)).astype(jnp.int32)
    block_mask = set_ends((jax.random.randint(keys[4], (LAYERS, SECTIONS, NB), 0, 4) < 3).astype(jnp.int32), jax.random.fold_in(keys[4], 1), 0, 1)
    ffn_gain = jnp.clip(1.0 + 0.15 * jax.random.normal(keys[5], (LAYERS, D), jnp.float32), 0.25, 1.75)
    ffn_in = normal_values(keys[6], (LAYERS, 2, D, FF), D ** -0.5, 0.21875, ((3, 16),))
    ffn_out = normal_values(keys[7], (LAYERS, D, FF), FF ** -0.5, 0.125, ((2, 16),))
    return {"recording": recording, "mix_gain": mix_gain, "block_weights": block_weights, "section_perm": section_perm, "block_mask": block_mask, "ffn_gain": ffn_gain, "ffn_in": ffn_in, "ffn_out": ffn_out}


epsilon = 1e-05

def rms_scale(values, gain):
    values = values.astype(jnp.float32)
    mean_sq = lax.optimization_barrier(jnp.mean(values * values, axis=-1, keepdims=True))
    return values * lax.rsqrt(mean_sq + epsilon) * gain

def reference(recording, mix_gain, block_weights, section_perm, block_mask, ffn_gain, ffn_in, ffn_out):
    total_bits = NB.bit_length() - 1

    def encode_token(token_frame):
        for layer_idx in range(LAYERS):
            normed = rms_scale(token_frame, mix_gain[layer_idx]).astype(jnp.bfloat16)
            blocks = normed.reshape(NB, BLK, D)
            for section_idx in range(SECTIONS):
                section_bit = total_bits - 1 - section_idx
                permuted = jnp.take(blocks, section_perm[layer_idx, section_idx], axis=1)
                partner_ids = jnp.arange(NB, dtype=jnp.int32) ^ 1 << section_bit
                partner = jnp.take(permuted, partner_ids, axis=0)
                weights = block_weights[layer_idx, section_idx].astype(jnp.float32)
                own_term = jnp.einsum('noi,nid->nod', weights[:, 0], permuted.astype(jnp.float32))
                far_term = jnp.einsum('noi,nid->nod', weights[:, 1], partner.astype(jnp.float32))
                gate_far = block_mask[layer_idx, section_idx].astype(jnp.float32)[:, None, None]
                blocks = (own_term + gate_far * far_term).astype(jnp.bfloat16)
            mixed = (token_frame.astype(jnp.float32) + blocks.reshape(CH, D).astype(jnp.float32)).astype(jnp.bfloat16)
            ffn_normed = rms_scale(mixed, ffn_gain[layer_idx]).astype(jnp.bfloat16)
            gate_proj = jnp.dot(ffn_normed, ffn_in[layer_idx, 0], preferred_element_type=jnp.float32)
            up_proj = jnp.dot(ffn_normed, ffn_in[layer_idx, 1], preferred_element_type=jnp.float32)
            hidden = (jax.nn.silu(gate_proj) * up_proj).astype(jnp.bfloat16)
            down_proj = lax.dot_general(hidden, ffn_out[layer_idx], (((1,), (1,)), ((), ())), preferred_element_type=jnp.float32)
            token_frame = (mixed.astype(jnp.float32) + down_proj).astype(jnp.bfloat16)
        return token_frame
    return lax.map(encode_token, recording)
```

```python
import functools

import jax
import jax.numpy as jnp
from jax import lax
from jax.experimental import pallas as pl
from jax.experimental.pallas import tpu as pltpu
from jax.sharding import PartitionSpec as P

epsilon = 1e-05
WINDOW = 4
OFFSETS = (0, 4, 7, 9)
RING = 8
FTILE = 512


def rms_scale(values, gain):
    values = values.astype(jnp.float32)
    mean_sq = jnp.mean(values * values, axis=-1, keepdims=True)
    return values * lax.rsqrt(mean_sq + epsilon) * gain


def mixing_kernel(
    dims,
    x_ref,
    gain1_ref,
    bw_ref,
    perm_ref,
    mask_ref,
    gain2_ref,
    wl_ref,
    out_ref,
    own0,
    ring,
    far,
    wc,
    wf,
    hn,
    acc,
    send_sem,
    recv_sem,
    ag_send,
    ag_recv,
    local_sem,
    out_sem,
):
    n_dev, sections, nb, batch, first_bit, split = dims
    chunks, blk, width = x_ref.shape
    hidden_units = wf.shape[1]
    shard = wl_ref.shape[1] // split
    n_batches = chunks // batch
    bits = n_dev.bit_length() - 1
    last = sections - 1
    me = lax.axis_index("mix")
    partners = [me + (1 << b) * (1 - 2 * ((me // (1 << b)) % 2)) for b in range(bits)]

    group = lax.axis_index("groups")
    sibling = group + 1 - 2 * (group % 2)
    targets = [{"mix": partners[b]} for b in range(bits)]
    if split == 2:
        targets = targets + [{"groups": sibling}]
    piece = pl.ds(pl.multiple_of((group % split) * shard, shard), shard)
    local = pltpu.make_async_copy(
        wl_ref.at[:, piece, :], wf.at[:, pl.ds(0, shard), :], local_sem
    )
    local.start()
    route = [targets[b] for b in range(bits - 1, 0, -1)] + targets[bits:] + targets[: min(bits, 1)]
    rounds = len(route)

    barrier = pltpu.get_barrier_semaphore()
    for target in targets:
        pl.semaphore_signal(
            barrier, inc=1, device_id=target, device_id_type=pl.DeviceIdType.MESH
        )
    pl.semaphore_wait(barrier, len(targets))

    def own_at(s, k):
        return own0.at[k] if s == 0 else ring.at[s - 1, k % RING]

    def exchange(s, k):
        return pltpu.make_async_remote_copy(
            src_ref=own_at(s, k),
            dst_ref=far.at[s, k],
            send_sem=send_sem.at[s, k],
            recv_sem=recv_sem.at[s, k],
            device_id={"mix": partners[first_bit - s]},
            device_id_type=pl.DeviceIdType.MESH,
        )

    def gather_step(g):
        count = shard << g
        return pltpu.make_async_remote_copy(
            src_ref=wf.at[:, pl.ds(0, count), :],
            dst_ref=wf.at[:, pl.ds(count, count), :],
            send_sem=ag_send.at[g],
            recv_sem=ag_recv.at[g],
            device_id=route[g],
            device_id_type=pl.DeviceIdType.MESH,
        )

    def norm_and_send(k):
        own0[k] = rms_scale(x_ref[k], gain1_ref[...]).astype(jnp.bfloat16)
        exchange(0, k).start()

    def first(k, carry):
        norm_and_send(k)
        return carry

    window = min(WINDOW, chunks)
    lax.fori_loop(0, window, first, 0)
    local.wait()
    if rounds:
        gather_step(0).start()

    def fold(q, carry):
        s = q // nb
        where_to = lax.broadcasted_iota(jnp.int32, (blk, blk), 1)
        hot = (perm_ref[s] == where_to).astype(jnp.float32).astype(jnp.bfloat16)
        keep = mask_ref[q].astype(jnp.float32)
        wc[q, :, :blk] = jnp.dot(
            bw_ref[q, 0], hot, preferred_element_type=jnp.float32
        ).astype(jnp.bfloat16)
        wc[q, :, blk:] = (
            keep * jnp.dot(bw_ref[q, 1], hot, preferred_element_type=jnp.float32)
        ).astype(jnp.bfloat16)
        return carry

    lax.fori_loop(0, sections * nb, fold, 0)

    def section(s, k):
        both = jnp.concatenate([own_at(s, k)[...], far[s, k]], axis=0)
        return jnp.dot(
            wc[s * nb + k % nb], both, preferred_element_type=jnp.float32
        ).astype(jnp.bfloat16)

    def ffn(b, carry):
        rows = batch * blk
        base = pl.multiple_of(b * batch, batch)
        mixed = own0[pl.ds(base, batch)].reshape(rows, width)
        hn[...] = rms_scale(mixed, gain2_ref[...]).astype(jnp.bfloat16)
        acc[...] = mixed.astype(jnp.float32)

        def tile(f, inner):
            at = pl.ds(pl.multiple_of(f * FTILE, FTILE), FTILE)
            nt = (((1,), (1,)), ((), ()))
            gate = lax.dot_general(hn[...], wf[0, at, :], nt, preferred_element_type=jnp.float32)
            up = lax.dot_general(hn[...], wf[1, at, :], nt, preferred_element_type=jnp.float32)
            hidden = (gate / (1.0 + jnp.exp(-gate)) * up).astype(jnp.bfloat16)
            acc[...] += jnp.dot(hidden, wf[2, at, :], preferred_element_type=jnp.float32)
            return inner

        lax.fori_loop(0, hidden_units // FTILE, tile, 0)
        own0[pl.ds(base, batch)] = acc[...].astype(jnp.bfloat16).reshape(batch, blk, width)
        pltpu.make_async_copy(
            own0.at[pl.ds(base, batch)], out_ref.at[pl.ds(base, batch)], out_sem.at[b]
        ).start()
        return carry

    ffn_from = 5 * chunks // 8 + 1
    gather_at = [1 + g * (ffn_from - 1) // max(rounds, 1) for g in range(rounds)]

    def ready(i):
        done = jnp.clip((i - OFFSETS[last] + 1) // batch, 0, n_batches)
        return jnp.where(i >= ffn_from, done, 0)

    def step(i, carry):
        for g in range(1, rounds):

            @pl.when(i == gather_at[g])
            def _(g=g):
                gather_step(g - 1).wait_recv()
                gather_step(g).start()

        @pl.when(i + window < chunks)
        def _():
            norm_and_send(i + window)

        for s in range(sections):
            k = i - OFFSETS[s]

            @pl.when(jnp.logical_and(k >= 0, k < chunks))
            def _(s=s, k=k):
                exchange(s, k).wait_recv()
                result = section(s, k)
                if s < last:

                    @pl.when(k >= RING)
                    def _():
                        exchange(s + 1, k - RING).wait_send()

                    own_at(s + 1, k)[...] = result
                    exchange(s + 1, k).start()
                else:
                    exchange(0, k).wait_send()
                    own0[k] = (
                        x_ref[k].astype(jnp.float32) + result.astype(jnp.float32)
                    ).astype(jnp.bfloat16)

        if rounds:

            @pl.when(i == ffn_from)
            def _():
                gather_step(rounds - 1).wait_recv()

        lax.fori_loop(ready(i - 1), ready(i), ffn, 0)
        return carry

    lax.fori_loop(0, chunks + OFFSETS[last], step, 0)

    for s in range(1, sections):
        for k in range(max(chunks - RING, 0), chunks):
            exchange(s, k).wait_send()
    for g in range(rounds):
        gather_step(g).wait_send()
    for b in range(n_batches):
        at = pl.ds(b * batch, batch)
        pltpu.make_async_copy(own0.at[at], out_ref.at[at], out_sem.at[b]).wait()


def exchanged(
    recording, mix_gain, block_weights, section_perm, block_mask, ffn_gain, ffn_in, ffn_out
):
    time_steps, local_ch, width = recording.shape
    sections, nb, _, blk, _ = block_weights.shape[1:]
    n_dev = lax.axis_size("mix")
    chunks = time_steps * nb
    batch = 4
    while chunks % batch:
        batch //= 2
    bits = n_dev.bit_length() - 1
    total_bits = (n_dev * nb).bit_length() - 1
    first_bit = total_bits - 1 - (nb.bit_length() - 1)
    shard = ffn_in.shape[-1]
    split = 2 if lax.axis_size("groups") % 2 == 0 and shard % 32 == 0 else 1
    rounds = bits + split - 1
    local_weights = jnp.concatenate(
        [jnp.swapaxes(ffn_in[0], 1, 2), jnp.swapaxes(ffn_out, 1, 2)], axis=0
    )
    vmem = pl.BlockSpec(memory_space=pltpu.VMEM)
    anywhere = pl.BlockSpec(memory_space=pl.ANY)
    result = pl.pallas_call(
        functools.partial(mixing_kernel, (n_dev, sections, nb, batch, first_bit, split)),
        out_shape=jax.ShapeDtypeStruct((chunks, blk, width), jnp.bfloat16),
        in_specs=[vmem, vmem, vmem, vmem, pl.BlockSpec(memory_space=pltpu.SMEM), vmem, anywhere],
        out_specs=anywhere,
        scratch_shapes=[
            pltpu.VMEM((chunks, blk, width), jnp.bfloat16),
            pltpu.VMEM((sections - 1, RING, blk, width), jnp.bfloat16),
            pltpu.VMEM((sections, chunks, blk, width), jnp.bfloat16),
            pltpu.VMEM((sections * nb, blk, 2 * blk), jnp.bfloat16),
            pltpu.VMEM((3, shard * n_dev, width), jnp.bfloat16),
            pltpu.VMEM((batch * blk, width), jnp.bfloat16),
            pltpu.VMEM((batch * blk, width), jnp.float32),
            pltpu.SemaphoreType.DMA((sections, chunks)),
            pltpu.SemaphoreType.DMA((sections, chunks)),
            pltpu.SemaphoreType.DMA((rounds,)),
            pltpu.SemaphoreType.DMA((rounds,)),
            pltpu.SemaphoreType.DMA,
            pltpu.SemaphoreType.DMA((chunks // batch,)),
        ],
        compiler_params=pltpu.CompilerParams(
            collective_id=0, has_side_effects=True, vmem_limit_bytes=60 * 1024 * 1024
        ),
    )(
        recording.reshape(chunks, blk, width),
        mix_gain,
        block_weights[0].reshape(sections * nb, 2, blk, blk),
        section_perm[0][:, :, None],
        block_mask[0].reshape(sections * nb),
        ffn_gain,
        local_weights,
    )
    return result.reshape(time_steps, local_ch, width)


LEAD = 4
OUTER_LEAD = 8
HALVES = 2
SLOTS = 8
STREAM = 4
BATCH = 4
GROUPED = 4


def relay_kernel(
    dims,
    x_ref,
    gain1_ref,
    bw_ref,
    perm_ref,
    mask_ref,
    gain2_ref,
    win_ref,
    wout_ref,
    out_ref,
    wf_out,
    own,
    fo,
    fc,
    fr,
    f2,
    f3,
    oring,
    vring,
    wc,
    wx,
    wf,
    hn,
    acc,
    xin,
    xres,
    send_sem,
    recv_sem,
    wx_send,
    wx_recv,
    ag_send,
    ag_recv,
    local_sem,
    xin_sem,
    xres_sem,
    out_sem,
    tail_sem,
    wf_sem,
):
    sections, nb = dims
    chunks, blk, width = x_ref.shape
    units = chunks * HALVES
    part = width // HALVES
    shards, wrows, _ = wf.shape
    half_rows = wrows // 2
    n_batches = chunks // BATCH
    VERTICAL, CROSS, RELAY, SIDE, CORE = range(5)

    me = lax.axis_index("mix")
    group = lax.axis_index("groups")
    shift = [(1 << b) * (1 - 2 * ((me // (1 << b)) % 2)) for b in range(4)]
    z = me // 4
    mid = jnp.logical_or(z == 1, z == 2)
    outer = jnp.logical_not(mid)
    far_z = {"mix": me + shift[3]}
    near_z = {"mix": me + shift[2]}
    cross_z = {"mix": me + shift[3] + shift[2]}
    side = {"mix": me + shift[1]}
    core = {"mix": me + shift[0]}
    sibling = {"groups": group + 1 - 2 * (group % 2)}
    half = group % 2

    def x_load(k):
        return pltpu.make_async_copy(x_ref.at[k], xin.at[k % STREAM], xin_sem.at[k % STREAM])

    def x_again(u):
        at = pl.ds(pl.multiple_of((u % HALVES) * part, part), part)
        return pltpu.make_async_copy(
            x_ref.at[u // HALVES, :, at], xres.at[u % STREAM], xres_sem.at[u % STREAM]
        )

    for k in range(STREAM):
        x_load(k).start()
    for u in range(STREAM):
        x_again(u).start()

    d_model = width
    first_half = [
        pltpu.make_async_copy(
            win_ref.at[0, 0], wf.at[0, pl.ds(0, d_model), :], local_sem.at[0]
        ),
        pltpu.make_async_copy(
            win_ref.at[0, 1, pl.ds(0, half_rows - d_model), :],
            wf.at[0, pl.ds(d_model, half_rows - d_model), :],
            local_sem.at[1],
        ),
    ]
    second_half = [
        pltpu.make_async_copy(
            win_ref.at[0, 1, pl.ds(half_rows - d_model, 2 * d_model - half_rows), :],
            wf.at[0, pl.ds(half_rows, 2 * d_model - half_rows), :],
            local_sem.at[0],
        ),
        pltpu.make_async_copy(
            wout_ref.at[0], wf.at[0, pl.ds(2 * d_model, d_model), :], local_sem.at[1]
        ),
    ]
    for which, copies in enumerate((first_half, second_half)):

        @pl.when(half == which)
        def _(copies=copies):
            for copy in copies:
                copy.start()

    barrier = pltpu.get_barrier_semaphore()
    targets = [far_z, near_z, cross_z, side, core, sibling]
    for target in targets:
        pl.semaphore_signal(
            barrier, inc=1, device_id=target, device_id_type=pl.DeviceIdType.MESH
        )
    pl.semaphore_wait(barrier, len(targets))

    def send(kind, u, src, dst, target):
        return pltpu.make_async_remote_copy(
            src_ref=src,
            dst_ref=dst,
            send_sem=send_sem.at[kind, u],
            recv_sem=recv_sem.at[kind, u],
            device_id=target,
            device_id_type=pl.DeviceIdType.MESH,
        )

    def up(u):
        return send(VERTICAL, u, own.at[u], fo.at[u], near_z)

    def down(u):
        return send(VERTICAL, u, oring.at[u % SLOTS], fo.at[u], near_z)

    def cross(u):
        return send(CROSS, u, own.at[u], fc.at[u], cross_z)

    def relay(u):
        return send(RELAY, u, fo.at[u], fr.at[u], cross_z)

    def sideways(u):
        return send(SIDE, u, own.at[u], f2.at[u], side)

    def cores(u):
        return send(CORE, u, vring.at[u % SLOTS], f3.at[u], core)

    rows = pl.ds(pl.multiple_of(half * half_rows, half_rows), half_rows)
    gathers = []
    for g, target in enumerate((far_z, near_z, side, sibling, core)):
        if g < 3:
            count = 1 << g
            src = wf.at[pl.ds(0, count), rows, :]
            dst = wf.at[pl.ds(count, count), rows, :]
        elif g == 3:
            src = dst = wf.at[pl.ds(0, shards // 2), rows, :]
        else:
            src = wf.at[pl.ds(0, shards // 2)]
            dst = wf.at[pl.ds(shards // 2, shards // 2)]
        gathers.append(
            pltpu.make_async_remote_copy(
                src_ref=src,
                dst_ref=dst,
                send_sem=ag_send.at[g],
                recv_sem=ag_recv.at[g],
                device_id=target,
                device_id_type=pl.DeviceIdType.MESH,
            )
        )

    for which, copies in enumerate((first_half, second_half)):

        @pl.when(half == which)
        def _(copies=copies):
            for copy in copies:
                copy.wait()

    gathers[0].start()

    def norm_and_send(k):
        x_load(k).wait()
        normed = rms_scale(xin[k % STREAM], gain1_ref[...]).astype(jnp.bfloat16)
        for h in range(HALVES):
            u = k * HALVES + h
            own[u] = normed[:, h * part : (h + 1) * part]

            @pl.when(mid)
            def _(u=u):
                cross(u).start()

            @pl.when(outer)
            def _(u=u):
                up(u).start()

        @pl.when(k + STREAM < chunks)
        def _():
            x_load(k + STREAM).start()

    def first(k, carry):
        norm_and_send(k)
        return carry

    def fold(q, carry):
        s = q // nb
        n = q % nb
        what = lax.broadcasted_iota(jnp.int32, (blk, blk), 0)
        hot = (perm_ref[0, pl.ds(s, 1), :] == what).astype(jnp.float32).astype(jnp.bfloat16)
        keep = mask_ref[0, s, n].astype(jnp.float32)
        nt = (((1,), (1,)), ((), ()))
        wc[q, :, :blk] = lax.dot_general(
            bw_ref[0, s, n, 0], hot, nt, preferred_element_type=jnp.float32
        ).astype(jnp.bfloat16)
        wc[q, :, blk:] = (
            keep
            * lax.dot_general(bw_ref[0, s, n, 1], hot, nt, preferred_element_type=jnp.float32)
        ).astype(jnp.bfloat16)
        return carry

    def lend(s):
        at = pl.ds(s * nb, nb)
        return pltpu.make_async_remote_copy(
            src_ref=wc.at[at],
            dst_ref=wx.at[at],
            send_sem=wx_send.at[s],
            recv_sem=wx_recv.at[s],
            device_id=near_z,
            device_id_type=pl.DeviceIdType.MESH,
        )

    lax.fori_loop(0, LEAD, first, 0)
    lax.fori_loop(0, 2 * nb, fold, 0)

    @pl.when(outer)
    def _():
        for s in range(2):
            lend(s).start()

    lax.fori_loop(2 * nb, sections * nb, fold, 0)

    @pl.when(outer)
    def _():
        lax.fori_loop(LEAD, OUTER_LEAD, first, 0)

    lead = jnp.where(mid, LEAD, OUTER_LEAD)

    def pass_on(u):
        up(u).wait_recv()
        relay(u).start()

    @pl.when(mid)
    def _():
        def early(u, carry):
            pass_on(u)
            return carry

        lax.fori_loop(0, LEAD * HALVES, early, 0)
        for s in range(2):
            lend(s).wait_recv()

    def mix(weights, a, b):
        return jnp.dot(
            weights, jnp.concatenate([a, b], axis=0), preferred_element_type=jnp.float32
        ).astype(jnp.bfloat16)

    def block_of(u):
        return (u // HALVES) % nb

    def both_sections(u):
        n = block_of(u)
        cross(u).wait_recv()
        mine = own[u]
        outs = fo[u]
        relay(u).wait_recv()
        y_out = mix(wx[n], outs, fc[u])
        y_own = mix(wc[n], mine, fr[u])

        @pl.when(u >= SLOTS)
        def _():
            down(u - SLOTS).wait_send()

        oring[u % SLOTS] = mix(wx[nb + n], y_out, y_own)
        down(u).start()
        cross(u).wait_send()
        own[u] = mix(wc[nb + n], y_own, y_out)
        sideways(u).start()

    def take_back(u):
        down(u).wait_recv()
        up(u).wait_send()
        own[u] = fo[u]
        sideways(u).start()

    def third(u):
        sideways(u).wait_recv()
        result = mix(wc[2 * nb + block_of(u)], own[u], f2[u])

        @pl.when(u >= SLOTS)
        def _():
            cores(u - SLOTS).wait_send()

        vring[u % SLOTS] = result
        cores(u).start()

    tail_units = BATCH * HALVES

    def tail_copy(u):
        at = pl.ds(pl.multiple_of((u % HALVES) * part, part), part)
        return pltpu.make_async_copy(
            own.at[u], out_ref.at[u // HALVES, :, at], tail_sem.at[u % tail_units]
        )

    def fourth(u):
        x_again(u).wait()
        cores(u).wait_recv()
        result = mix(wc[3 * nb + block_of(u)], vring[u % SLOTS], f3[u])
        sideways(u).wait_send()
        own[u] = (
            xres[u % STREAM].astype(jnp.float32) + result.astype(jnp.float32)
        ).astype(jnp.bfloat16)

        @pl.when(u + STREAM < units)
        def _():
            x_again(u + STREAM).start()

        @pl.when(u >= units - tail_units)
        def _():
            tail_copy(u).start()

    def out_copies(b):
        return [
            pltpu.make_async_copy(
                hn.at[j],
                out_ref.at[b * BATCH + j],
                out_sem.at[j],
            )
            for j in range(BATCH)
        ]

    def ffn(b):
        @pl.when(b > 0)
        def _():
            for copy in out_copies(b - 1):
                copy.wait()

        def get(j, carry):
            base = (b * BATCH + j) * HALVES
            mixed = jnp.concatenate([own[base + h] for h in range(HALVES)], axis=1)
            hn[j] = rms_scale(mixed, gain2_ref[...]).astype(jnp.bfloat16)
            acc[j] = mixed.astype(jnp.float32)
            return carry

        lax.fori_loop(0, BATCH, get, 0)

        def tile(f, carry):
            normed = hn[...].reshape(BATCH * blk, width)
            base = f * GROUPED

            def weights(which):
                at = pl.ds(which * width, width)
                return jnp.concatenate([wf[base + j, at, :] for j in range(GROUPED)], axis=1)

            gate = jnp.dot(normed, weights(0), preferred_element_type=jnp.float32)
            up_part = jnp.dot(normed, weights(1), preferred_element_type=jnp.float32)
            hidden = (gate / (1.0 + jnp.exp(-gate)) * up_part).astype(jnp.bfloat16)
            acc[...] += lax.dot_general(
                hidden, weights(2), (((1,), (1,)), ((), ())), preferred_element_type=jnp.float32
            ).reshape(BATCH, blk, width)
            return carry

        lax.fori_loop(0, shards // GROUPED, tile, 0)
        hn[...] = acc[...].astype(jnp.bfloat16)
        for copy in out_copies(b):
            copy.start()

    gather_at = [0, 4 * HALVES, 8 * HALVES, 11 * HALVES, 18 * HALVES]
    ffn_from = 20 * HALVES
    wf_copy = pltpu.make_async_copy(wf, wf_out, wf_sem)
    late = jnp.where(mid, 0, 2)

    def ready(i):
        finished = (i - (late + 4) + 1) // tail_units
        turn = (i - ffn_from) // HALVES + 1
        return jnp.clip(jnp.minimum(finished, turn), 0, n_batches - 1)

    def within(u):
        return jnp.logical_and(u >= 0, u < units)

    def step(i, carry):
        for g in range(1, 5):

            @pl.when(i == gather_at[g])
            def _(g=g):
                gathers[g - 1].wait_recv()
                gathers[g].start()

        @pl.when(i == ffn_from)
        def _():
            gathers[4].wait_recv()
            wf_copy.start()

        @pl.when(jnp.logical_and(i % HALVES == 0, i // HALVES + lead < chunks))
        def _():
            norm_and_send(i // HALVES + lead)

        @pl.when(mid)
        def _():
            @pl.when(i + LEAD * HALVES < units)
            def _():
                pass_on(i + LEAD * HALVES)

            @pl.when(i < units)
            def _():
                both_sections(i)

        @pl.when(jnp.logical_and(outer, within(i - late)))
        def _():
            take_back(i - late)

        @pl.when(within(i - late - 2))
        def _():
            third(i - late - 2)

        @pl.when(within(i - late - 4))
        def _():
            fourth(i - late - 4)

        @pl.when(ready(i) > ready(i - 1))
        def _():
            ffn(ready(i) - 1)

        return carry

    lax.fori_loop(0, units + 6, step, 0)

    @pl.when(mid)
    def _():
        def relays(u, carry):
            relay(u).wait_send()
            return carry

        lax.fori_loop(0, units, relays, 0)

        def downs(u, carry):
            down(u).wait_send()
            return carry

        lax.fori_loop(units - SLOTS, units, downs, 0)

    @pl.when(outer)
    def _():
        for s in range(2):
            lend(s).wait_send()

    def lasts(u, carry):
        cores(u).wait_send()
        return carry

    lax.fori_loop(units - SLOTS, units, lasts, 0)
    for gather in gathers:
        gather.wait_send()
    for copy in out_copies(n_batches - 2):
        copy.wait()

    def tails(u, carry):
        tail_copy(u).wait()
        return carry

    lax.fori_loop(units - tail_units, units, tails, 0)
    wf_copy.wait()


def finish_kernel(
    done_ref, gain2_ref, wf_ref, out_ref, wf, mixed_ref, hn, acc, in_sem, wf_sem, copy_sem, out_sem
):
    chunks, blk, width = done_ref.shape
    shards = wf_ref.shape[0]
    tiles = shards // GROUPED
    head = chunks - BATCH
    load = pltpu.make_async_copy(done_ref.at[pl.ds(head, BATCH)], mixed_ref, in_sem)
    load.start()
    loads = []
    for f in range(tiles):
        at = pl.ds(f * GROUPED, GROUPED)
        loads.append(pltpu.make_async_copy(wf_ref.at[at], wf.at[at], wf_sem.at[f]))
    copies = []
    for p in range(head // BATCH):
        at = pl.ds(p * BATCH, BATCH)
        copies.append(pltpu.make_async_copy(done_ref.at[at], out_ref.at[at], copy_sem.at[p]))
    loads[0].start()
    loads[1].start()
    for copy in copies:
        copy.start()
    for copy in loads[2:]:
        copy.start()
    load.wait()
    mixed = mixed_ref[...].reshape(BATCH * blk, width)
    hn[...] = rms_scale(mixed, gain2_ref[...]).astype(jnp.bfloat16)
    acc[...] = mixed.astype(jnp.float32)
    for f in range(tiles):
        loads[f].wait()

        def weights(which):
            at = pl.ds(which * width, width)
            return jnp.concatenate(
                [wf[f * GROUPED + j, at, :] for j in range(GROUPED)], axis=1
            )

        gate = jnp.dot(hn[...], weights(0), preferred_element_type=jnp.float32)
        up_part = jnp.dot(hn[...], weights(1), preferred_element_type=jnp.float32)
        hidden = (gate / (1.0 + jnp.exp(-gate)) * up_part).astype(jnp.bfloat16)
        acc[...] += lax.dot_general(
            hidden, weights(2), (((1,), (1,)), ((), ())), preferred_element_type=jnp.float32
        )
    mixed_ref[...] = acc[...].astype(jnp.bfloat16).reshape(BATCH, blk, width)
    store = pltpu.make_async_copy(mixed_ref, out_ref.at[pl.ds(head, BATCH)], out_sem)
    store.start()
    for copy in copies:
        copy.wait()
    store.wait()


def relayed(
    recording, mix_gain, block_weights, section_perm, block_mask, ffn_gain, ffn_in, ffn_out
):
    time_steps, local_ch, width = recording.shape
    sections, nb, _, blk, _ = block_weights.shape[1:]
    chunks = time_steps * nb
    units = chunks * HALVES
    part = width // HALVES
    shard = ffn_in.shape[-1]
    shards = lax.axis_size("mix")
    vmem = pl.BlockSpec(memory_space=pltpu.VMEM)
    smem = pl.BlockSpec(memory_space=pltpu.SMEM)
    anywhere = pl.BlockSpec(memory_space=pl.ANY)
    far = pltpu.VMEM((units, blk, part), jnp.bfloat16)
    ring = pltpu.VMEM((SLOTS, blk, part), jnp.bfloat16)
    done, weights = pl.pallas_call(
        functools.partial(relay_kernel, (sections, nb)),
        out_shape=(
            jax.ShapeDtypeStruct((chunks, blk, width), jnp.bfloat16),
            jax.ShapeDtypeStruct((shards, 3 * width, shard), jnp.bfloat16),
        ),
        in_specs=[anywhere, vmem, vmem, vmem, smem, vmem, anywhere, anywhere],
        out_specs=(anywhere, anywhere),
        scratch_shapes=[far] * 6
        + [ring] * 2
        + [
            pltpu.VMEM((sections * nb, blk, 2 * blk), jnp.bfloat16),
            pltpu.VMEM((2 * nb, blk, 2 * blk), jnp.bfloat16),
            pltpu.VMEM((shards, 3 * width, shard), jnp.bfloat16),
            pltpu.VMEM((BATCH, blk, width), jnp.bfloat16),
            pltpu.VMEM((BATCH, blk, width), jnp.float32),
            pltpu.VMEM((STREAM, blk, width), jnp.bfloat16),
            pltpu.VMEM((STREAM, blk, part), jnp.bfloat16),
            pltpu.SemaphoreType.DMA((5, units)),
            pltpu.SemaphoreType.DMA((5, units)),
            pltpu.SemaphoreType.DMA((2,)),
            pltpu.SemaphoreType.DMA((2,)),
            pltpu.SemaphoreType.DMA((5,)),
            pltpu.SemaphoreType.DMA((5,)),
            pltpu.SemaphoreType.DMA((2,)),
            pltpu.SemaphoreType.DMA((STREAM,)),
            pltpu.SemaphoreType.DMA((STREAM,)),
            pltpu.SemaphoreType.DMA((BATCH,)),
            pltpu.SemaphoreType.DMA((BATCH * HALVES,)),
            pltpu.SemaphoreType.DMA,
        ],
        compiler_params=pltpu.CompilerParams(
            collective_id=1, has_side_effects=True, vmem_limit_bytes=62 * 1024 * 1024
        ),
    )(
        recording.reshape(chunks, blk, width),
        mix_gain,
        block_weights,
        section_perm,
        block_mask,
        ffn_gain,
        ffn_in,
        ffn_out,
    )
    result = pl.pallas_call(
        finish_kernel,
        out_shape=jax.ShapeDtypeStruct((chunks, blk, width), jnp.bfloat16),
        in_specs=[anywhere, vmem, anywhere],
        out_specs=anywhere,
        scratch_shapes=[
            pltpu.VMEM((shards, 3 * width, shard), jnp.bfloat16),
            pltpu.VMEM((BATCH, blk, width), jnp.bfloat16),
            pltpu.VMEM((BATCH * blk, width), jnp.bfloat16),
            pltpu.VMEM((BATCH * blk, width), jnp.float32),
            pltpu.SemaphoreType.DMA,
            pltpu.SemaphoreType.DMA((shards // GROUPED,)),
            pltpu.SemaphoreType.DMA((chunks // BATCH - 1,)),
            pltpu.SemaphoreType.DMA,
        ],
        compiler_params=pltpu.CompilerParams(vmem_limit_bytes=40 * 1024 * 1024),
    )(done, ffn_gain, weights)
    return result.reshape(time_steps, local_ch, width)


def on_device(recording, mix_gain, block_weights, *rest):
    sections, nb = block_weights.shape[1:3]
    chunks = recording.shape[0] * nb
    fits = (
        lax.axis_size("mix") == 16
        and lax.axis_size("groups") % 2 == 0
        and sections == 4
        and chunks % BATCH == 0
        and chunks >= 32
    )
    plan = relayed if fits else exchanged
    return plan(recording, mix_gain, block_weights, *rest)


def solution(mesh):
    in_specs = (
        P("groups", "mix", None),
        P(),
        P(None, None, "mix", None, None, None),
        P(),
        P(None, None, "mix"),
        P(),
        P(None, None, None, "mix"),
        P(None, None, "mix"),
    )
    out_specs = P("groups", "mix", None)
    return jax.shard_map(
        on_device, mesh=mesh, in_specs=in_specs, out_specs=out_specs, check_vma=False
    )
```

```python
import functools

import jax
import jax.numpy as jnp
from jax import lax
from jax.experimental import pallas as pl
from jax.experimental.pallas import tpu as pltpu
from jax.sharding import PartitionSpec as P

epsilon = 1e-05
WINDOW = 4
OFFSETS = (0, 4, 7, 9)
RING = 8
FTILE = 512


def rms_scale(values, gain):
    values = values.astype(jnp.float32)
    mean_sq = jnp.mean(values * values, axis=-1, keepdims=True)
    return values * lax.rsqrt(mean_sq + epsilon) * gain


def mixing_kernel(
    dims,
    x_ref,
    gain1_ref,
    bw_ref,
    perm_ref,
    mask_ref,
    gain2_ref,
    wl_ref,
    out_ref,
    own0,
    ring,
    far,
    wc,
    wf,
    hn,
    acc,
    send_sem,
    recv_sem,
    ag_send,
    ag_recv,
    local_sem,
    out_sem,
):
    n_dev, sections, nb, batch, first_bit, split = dims
    chunks, blk, width = x_ref.shape
    hidden_units = wf.shape[1]
    shard = wl_ref.shape[1] // split
    n_batches = chunks // batch
    bits = n_dev.bit_length() - 1
    last = sections - 1
    me = lax.axis_index("mix")
    partners = [me + (1 << b) * (1 - 2 * ((me // (1 << b)) % 2)) for b in range(bits)]

    group = lax.axis_index("groups")
    sibling = group + 1 - 2 * (group % 2)
    targets = [{"mix": partners[b]} for b in range(bits)]
    if split == 2:
        targets = targets + [{"groups": sibling}]
    piece = pl.ds(pl.multiple_of((group % split) * shard, shard), shard)
    local = pltpu.make_async_copy(
        wl_ref.at[:, piece, :], wf.at[:, pl.ds(0, shard), :], local_sem
    )
    local.start()
    route = [targets[b] for b in range(bits - 1, 0, -1)] + targets[bits:] + targets[: min(bits, 1)]
    rounds = len(route)

    barrier = pltpu.get_barrier_semaphore()
    for target in targets:
        pl.semaphore_signal(
            barrier, inc=1, device_id=target, device_id_type=pl.DeviceIdType.MESH
        )
    pl.semaphore_wait(barrier, len(targets))

    def own_at(s, k):
        return own0.at[k] if s == 0 else ring.at[s - 1, k % RING]

    def exchange(s, k):
        return pltpu.make_async_remote_copy(
            src_ref=own_at(s, k),
            dst_ref=far.at[s, k],
            send_sem=send_sem.at[s, k],
            recv_sem=recv_sem.at[s, k],
            device_id={"mix": partners[first_bit - s]},
            device_id_type=pl.DeviceIdType.MESH,
        )

    def gather_step(g):
        count = shard << g
        return pltpu.make_async_remote_copy(
            src_ref=wf.at[:, pl.ds(0, count), :],
            dst_ref=wf.at[:, pl.ds(count, count), :],
            send_sem=ag_send.at[g],
            recv_sem=ag_recv.at[g],
            device_id=route[g],
            device_id_type=pl.DeviceIdType.MESH,
        )

    def norm_and_send(k):
        own0[k] = rms_scale(x_ref[k], gain1_ref[...]).astype(jnp.bfloat16)
        exchange(0, k).start()

    def first(k, carry):
        norm_and_send(k)
        return carry

    window = min(WINDOW, chunks)
    lax.fori_loop(0, window, first, 0)
    local.wait()
    if rounds:
        gather_step(0).start()

    def fold(q, carry):
        s = q // nb
        where_to = lax.broadcasted_iota(jnp.int32, (blk, blk), 1)
        hot = (perm_ref[s] == where_to).astype(jnp.float32).astype(jnp.bfloat16)
        keep = mask_ref[q].astype(jnp.float32)
        wc[q, :, :blk] = jnp.dot(
            bw_ref[q, 0], hot, preferred_element_type=jnp.float32
        ).astype(jnp.bfloat16)
        wc[q, :, blk:] = (
            keep * jnp.dot(bw_ref[q, 1], hot, preferred_element_type=jnp.float32)
        ).astype(jnp.bfloat16)
        return carry

    lax.fori_loop(0, sections * nb, fold, 0)

    def section(s, k):
        both = jnp.concatenate([own_at(s, k)[...], far[s, k]], axis=0)
        return jnp.dot(
            wc[s * nb + k % nb], both, preferred_element_type=jnp.float32
        ).astype(jnp.bfloat16)

    def ffn(b, carry):
        rows = batch * blk
        base = pl.multiple_of(b * batch, batch)
        mixed = own0[pl.ds(base, batch)].reshape(rows, width)
        hn[...] = rms_scale(mixed, gain2_ref[...]).astype(jnp.bfloat16)
        acc[...] = mixed.astype(jnp.float32)

        def tile(f, inner):
            at = pl.ds(pl.multiple_of(f * FTILE, FTILE), FTILE)
            nt = (((1,), (1,)), ((), ()))
            gate = lax.dot_general(hn[...], wf[0, at, :], nt, preferred_element_type=jnp.float32)
            up = lax.dot_general(hn[...], wf[1, at, :], nt, preferred_element_type=jnp.float32)
            hidden = (gate / (1.0 + jnp.exp(-gate)) * up).astype(jnp.bfloat16)
            acc[...] += jnp.dot(hidden, wf[2, at, :], preferred_element_type=jnp.float32)
            return inner

        lax.fori_loop(0, hidden_units // FTILE, tile, 0)
        own0[pl.ds(base, batch)] = acc[...].astype(jnp.bfloat16).reshape(batch, blk, width)
        pltpu.make_async_copy(
            own0.at[pl.ds(base, batch)], out_ref.at[pl.ds(base, batch)], out_sem.at[b]
        ).start()
        return carry

    ffn_from = 5 * chunks // 8 + 1
    gather_at = [1 + g * (ffn_from - 1) // max(rounds, 1) for g in range(rounds)]

    def ready(i):
        done = jnp.clip((i - OFFSETS[last] + 1) // batch, 0, n_batches)
        return jnp.where(i >= ffn_from, done, 0)

    def step(i, carry):
        for g in range(1, rounds):

            @pl.when(i == gather_at[g])
            def _(g=g):
                gather_step(g - 1).wait_recv()
                gather_step(g).start()

        @pl.when(i + window < chunks)
        def _():
            norm_and_send(i + window)

        for s in range(sections):
            k = i - OFFSETS[s]

            @pl.when(jnp.logical_and(k >= 0, k < chunks))
            def _(s=s, k=k):
                exchange(s, k).wait_recv()
                result = section(s, k)
                if s < last:

                    @pl.when(k >= RING)
                    def _():
                        exchange(s + 1, k - RING).wait_send()

                    own_at(s + 1, k)[...] = result
                    exchange(s + 1, k).start()
                else:
                    exchange(0, k).wait_send()
                    own0[k] = (
                        x_ref[k].astype(jnp.float32) + result.astype(jnp.float32)
                    ).astype(jnp.bfloat16)

        if rounds:

            @pl.when(i == ffn_from)
            def _():
                gather_step(rounds - 1).wait_recv()

        lax.fori_loop(ready(i - 1), ready(i), ffn, 0)
        return carry

    lax.fori_loop(0, chunks + OFFSETS[last], step, 0)

    for s in range(1, sections):
        for k in range(max(chunks - RING, 0), chunks):
            exchange(s, k).wait_send()
    for g in range(rounds):
        gather_step(g).wait_send()
    for b in range(n_batches):
        at = pl.ds(b * batch, batch)
        pltpu.make_async_copy(own0.at[at], out_ref.at[at], out_sem.at[b]).wait()


def exchanged(
    recording, mix_gain, block_weights, section_perm, block_mask, ffn_gain, ffn_in, ffn_out
):
    time_steps, local_ch, width = recording.shape
    sections, nb, _, blk, _ = block_weights.shape[1:]
    n_dev = lax.axis_size("mix")
    chunks = time_steps * nb
    batch = 4
    while chunks % batch:
        batch //= 2
    bits = n_dev.bit_length() - 1
    total_bits = (n_dev * nb).bit_length() - 1
    first_bit = total_bits - 1 - (nb.bit_length() - 1)
    shard = ffn_in.shape[-1]
    split = 2 if lax.axis_size("groups") % 2 == 0 and shard % 32 == 0 else 1
    rounds = bits + split - 1
    local_weights = jnp.concatenate(
        [jnp.swapaxes(ffn_in[0], 1, 2), jnp.swapaxes(ffn_out, 1, 2)], axis=0
    )
    vmem = pl.BlockSpec(memory_space=pltpu.VMEM)
    anywhere = pl.BlockSpec(memory_space=pl.ANY)
    result = pl.pallas_call(
        functools.partial(mixing_kernel, (n_dev, sections, nb, batch, first_bit, split)),
        out_shape=jax.ShapeDtypeStruct((chunks, blk, width), jnp.bfloat16),
        in_specs=[vmem, vmem, vmem, vmem, pl.BlockSpec(memory_space=pltpu.SMEM), vmem, anywhere],
        out_specs=anywhere,
        scratch_shapes=[
            pltpu.VMEM((chunks, blk, width), jnp.bfloat16),
            pltpu.VMEM((sections - 1, RING, blk, width), jnp.bfloat16),
            pltpu.VMEM((sections, chunks, blk, width), jnp.bfloat16),
            pltpu.VMEM((sections * nb, blk, 2 * blk), jnp.bfloat16),
            pltpu.VMEM((3, shard * n_dev, width), jnp.bfloat16),
            pltpu.VMEM((batch * blk, width), jnp.bfloat16),
            pltpu.VMEM((batch * blk, width), jnp.float32),
            pltpu.SemaphoreType.DMA((sections, chunks)),
            pltpu.SemaphoreType.DMA((sections, chunks)),
            pltpu.SemaphoreType.DMA((rounds,)),
            pltpu.SemaphoreType.DMA((rounds,)),
            pltpu.SemaphoreType.DMA,
            pltpu.SemaphoreType.DMA((chunks // batch,)),
        ],
        compiler_params=pltpu.CompilerParams(
            collective_id=0, has_side_effects=True, vmem_limit_bytes=60 * 1024 * 1024
        ),
    )(
        recording.reshape(chunks, blk, width),
        mix_gain,
        block_weights[0].reshape(sections * nb, 2, blk, blk),
        section_perm[0][:, :, None],
        block_mask[0].reshape(sections * nb),
        ffn_gain,
        local_weights,
    )
    return result.reshape(time_steps, local_ch, width)


LEAD = 6
OUTER_LEAD = 10
HALVES = 2
SLOTS = 8
STREAM = 4
BATCH = 2
GROUPED = 4
LAG = 2


def mlp(hn, wf, acc):
    tiles = wf.shape[0] // GROUPED
    width = wf.shape[1] // 3

    def weights(f, which):
        at = pl.ds(which * width, width)
        return jnp.concatenate([wf[f * GROUPED + j, at, :] for j in range(GROUPED)], axis=1)

    def inner(f):
        gate = jnp.dot(hn[...], weights(f, 0), preferred_element_type=jnp.float32)
        up_part = jnp.dot(hn[...], weights(f, 1), preferred_element_type=jnp.float32)
        return (gate / (1.0 + jnp.exp(-gate)) * up_part).astype(jnp.bfloat16)

    hidden = inner(0)
    for f in range(tiles):
        later = inner(f + 1) if f + 1 < tiles else None
        acc[...] += lax.dot_general(
            hidden, weights(f, 2), (((1,), (1,)), ((), ())), preferred_element_type=jnp.float32
        )
        hidden = later


def relay_kernel(
    dims,
    x_ref,
    gain1_ref,
    bw_ref,
    perm_ref,
    mask_ref,
    gain2_ref,
    win_ref,
    wout_ref,
    own,
    wf,
    fo,
    fc,
    fr,
    f2,
    f3,
    oring,
    vring,
    wc,
    wx,
    bw,
    hn,
    acc,
    xin,
    xres,
    send_sem,
    recv_sem,
    wx_send,
    wx_recv,
    ag_send,
    ag_recv,
    local_sem,
    xin_sem,
    xres_sem,
    bw_sem,
):
    sections, nb = dims
    chunks, blk, width = x_ref.shape
    units = chunks * HALVES
    part = width // HALVES
    shards, wrows, _ = wf.shape
    half_rows = wrows // 2
    n_batches = chunks // BATCH
    VERTICAL, CROSS, RELAY, SIDE, CORE = range(5)

    me = lax.axis_index("mix")
    group = lax.axis_index("groups")
    shift = [(1 << b) * (1 - 2 * ((me // (1 << b)) % 2)) for b in range(4)]
    z = me // 4
    mid = jnp.logical_or(z == 1, z == 2)
    outer = jnp.logical_not(mid)
    far_z = {"mix": me + shift[3]}
    near_z = {"mix": me + shift[2]}
    cross_z = {"mix": me + shift[3] + shift[2]}
    side = {"mix": me + shift[1]}
    core = {"mix": me + shift[0]}
    sibling = {"groups": group + 1 - 2 * (group % 2)}
    half = group % 2

    def x_load(k):
        return pltpu.make_async_copy(x_ref.at[k], xin.at[k % STREAM], xin_sem.at[k % STREAM])

    def x_again(u):
        at = pl.ds(pl.multiple_of((u % HALVES) * part, part), part)
        return pltpu.make_async_copy(
            x_ref.at[u // HALVES, :, at], xres.at[u % STREAM], xres_sem.at[u % STREAM]
        )

    bw_load = pltpu.make_async_copy(bw_ref, bw, bw_sem)
    d_model = width
    first_half = [
        pltpu.make_async_copy(
            win_ref.at[0, 0], wf.at[0, pl.ds(0, d_model), :], local_sem.at[0]
        ),
        pltpu.make_async_copy(
            win_ref.at[0, 1, pl.ds(0, half_rows - d_model), :],
            wf.at[0, pl.ds(d_model, half_rows - d_model), :],
            local_sem.at[1],
        ),
    ]
    second_half = [
        pltpu.make_async_copy(
            win_ref.at[0, 1, pl.ds(half_rows - d_model, 2 * d_model - half_rows), :],
            wf.at[0, pl.ds(half_rows, 2 * d_model - half_rows), :],
            local_sem.at[0],
        ),
        pltpu.make_async_copy(
            wout_ref.at[0], wf.at[0, pl.ds(2 * d_model, d_model), :], local_sem.at[1]
        ),
    ]
    barrier = pltpu.get_barrier_semaphore()
    targets = [far_z, near_z, cross_z, side, core, sibling]
    for target in targets:
        pl.semaphore_signal(
            barrier, inc=1, device_id=target, device_id_type=pl.DeviceIdType.MESH
        )

    for which, copies in enumerate((first_half, second_half)):

        @pl.when(half == which)
        def _(copies=copies):
            for copy in copies:
                copy.start()

    for k in range(STREAM):
        x_load(k).start()
    bw_load.start()
    for u in range(STREAM):
        x_again(u).start()
    pl.semaphore_wait(barrier, len(targets))

    def send(kind, u, src, dst, target):
        return pltpu.make_async_remote_copy(
            src_ref=src,
            dst_ref=dst,
            send_sem=send_sem.at[kind, u],
            recv_sem=recv_sem.at[kind, u],
            device_id=target,
            device_id_type=pl.DeviceIdType.MESH,
        )

    def own_at(u):
        return own.at[u // HALVES, u % HALVES]

    def up(u):
        return send(VERTICAL, u, own_at(u), fo.at[u], near_z)

    def down(u):
        return send(VERTICAL, u, oring.at[u % SLOTS], fo.at[u], near_z)

    def cross(u):
        return send(CROSS, u, own_at(u), fc.at[u], cross_z)

    def relay(u):
        return send(RELAY, u, fo.at[u], fr.at[u], cross_z)

    def sideways(u):
        return send(SIDE, u, own_at(u), f2.at[u], side)

    def cores(u):
        return send(CORE, u, vring.at[u % SLOTS], f3.at[u], core)

    rows = pl.ds(pl.multiple_of(half * half_rows, half_rows), half_rows)
    gathers = []
    for g, target in enumerate((far_z, near_z, side, sibling, core)):
        if g < 3:
            count = 1 << g
            src = wf.at[pl.ds(0, count), rows, :]
            dst = wf.at[pl.ds(count, count), rows, :]
        elif g == 3:
            src = dst = wf.at[pl.ds(0, shards // 2), rows, :]
        else:
            src = wf.at[pl.ds(0, shards // 2)]
            dst = wf.at[pl.ds(shards // 2, shards // 2)]
        gathers.append(
            pltpu.make_async_remote_copy(
                src_ref=src,
                dst_ref=dst,
                send_sem=ag_send.at[g],
                recv_sem=ag_recv.at[g],
                device_id=target,
                device_id_type=pl.DeviceIdType.MESH,
            )
        )

    for which, copies in enumerate((first_half, second_half)):

        @pl.when(half == which)
        def _(copies=copies):
            for copy in copies:
                copy.wait()

    gathers[0].start()

    def norm_and_send(k):
        x_load(k).wait()
        normed = rms_scale(xin[k % STREAM], gain1_ref[...]).astype(jnp.bfloat16)
        for h in range(HALVES):
            u = k * HALVES + h
            own[k, h] = normed[:, h * part : (h + 1) * part]

            @pl.when(mid)
            def _(u=u):
                cross(u).start()

            @pl.when(outer)
            def _(u=u):
                up(u).start()

        @pl.when(k + STREAM < chunks)
        def _():
            x_load(k + STREAM).start()

    def first(k, carry):
        norm_and_send(k)
        return carry

    def fold(q, carry):
        s = q // nb
        n = q % nb
        what = lax.broadcasted_iota(jnp.int32, (blk, blk), 0)
        hot = (perm_ref[0, pl.ds(s, 1), :] == what).astype(jnp.float32).astype(jnp.bfloat16)
        keep = mask_ref[0, s, n].astype(jnp.float32)
        nt = (((1,), (1,)), ((), ()))
        wc[q, :, :blk] = lax.dot_general(
            bw[0, s, n, 0], hot, nt, preferred_element_type=jnp.float32
        ).astype(jnp.bfloat16)
        wc[q, :, blk:] = (
            keep
            * lax.dot_general(bw[0, s, n, 1], hot, nt, preferred_element_type=jnp.float32)
        ).astype(jnp.bfloat16)
        return carry

    def lend(s):
        at = pl.ds(s * nb, nb)
        return pltpu.make_async_remote_copy(
            src_ref=wc.at[at],
            dst_ref=wx.at[at],
            send_sem=wx_send.at[s],
            recv_sem=wx_recv.at[s],
            device_id=near_z,
            device_id_type=pl.DeviceIdType.MESH,
        )

    lax.fori_loop(0, LEAD, first, 0)
    bw_load.wait()
    lax.fori_loop(0, 2 * nb, fold, 0)

    @pl.when(outer)
    def _():
        for s in range(2):
            lend(s).start()

    lax.fori_loop(2 * nb, sections * nb, fold, 0)

    @pl.when(outer)
    def _():
        lax.fori_loop(LEAD, OUTER_LEAD, first, 0)

    lead = jnp.where(mid, LEAD, OUTER_LEAD)

    def pass_on(u):
        up(u).wait_recv()
        relay(u).start()

    @pl.when(mid)
    def _():
        def early(u, carry):
            pass_on(u)
            return carry

        lax.fori_loop(0, LEAD * HALVES, early, 0)
        for s in range(2):
            lend(s).wait_recv()

    def mix(weights, a, b):
        return jnp.dot(
            weights, jnp.concatenate([a, b], axis=0), preferred_element_type=jnp.float32
        ).astype(jnp.bfloat16)

    def block_of(u):
        return (u // HALVES) % nb

    def both_sections(u):
        n = block_of(u)
        cross(u).wait_recv()
        mine = own[u // HALVES, u % HALVES]
        outs = fo[u]
        relay(u).wait_recv()
        y_out = mix(wx[n], outs, fc[u])
        y_own = mix(wc[n], mine, fr[u])

        @pl.when(u >= SLOTS)
        def _():
            down(u - SLOTS).wait_send()

        oring[u % SLOTS] = mix(wx[nb + n], y_out, y_own)
        down(u).start()
        cross(u).wait_send()
        own[u // HALVES, u % HALVES] = mix(wc[nb + n], y_own, y_out)
        sideways(u).start()

    def take_back(u):
        down(u).wait_recv()
        up(u).wait_send()
        own[u // HALVES, u % HALVES] = fo[u]
        sideways(u).start()

    def third(u):
        sideways(u).wait_recv()
        result = mix(wc[2 * nb + block_of(u)], own[u // HALVES, u % HALVES], f2[u])

        @pl.when(u >= SLOTS)
        def _():
            cores(u - SLOTS).wait_send()

        vring[u % SLOTS] = result
        cores(u).start()

    def fourth(u):
        x_again(u).wait()
        cores(u).wait_recv()
        result = mix(wc[3 * nb + block_of(u)], vring[u % SLOTS], f3[u])
        sideways(u).wait_send()
        own[u // HALVES, u % HALVES] = (
            xres[u % STREAM].astype(jnp.float32) + result.astype(jnp.float32)
        ).astype(jnp.bfloat16)

        @pl.when(u + STREAM < units)
        def _():
            x_again(u + STREAM).start()

    def ffn(b):
        def get(j, carry):
            k = b * BATCH + j
            mixed = jnp.concatenate([own[k, h] for h in range(HALVES)], axis=1)
            at = pl.ds(pl.multiple_of(j * blk, blk), blk)
            hn[at] = rms_scale(mixed, gain2_ref[...]).astype(jnp.bfloat16)
            acc[at] = mixed.astype(jnp.float32)
            return carry

        lax.fori_loop(0, BATCH, get, 0)
        mlp(hn, wf, acc)
        for h in range(HALVES):
            own[pl.ds(b * BATCH, BATCH), h] = (
                acc[:, h * part : (h + 1) * part].astype(jnp.bfloat16).reshape(BATCH, blk, part)
            )

    gather_at = [0, 4 * HALVES, 8 * HALVES, 11 * HALVES, 18 * HALVES]
    ffn_from = 20 * HALVES
    late = jnp.where(mid, 0, LAG)
    batch_units = BATCH * HALVES

    def ready(i):
        finished = (i - (late + 2 * LAG) + 1) // batch_units
        turn = i - ffn_from + 1
        return jnp.clip(jnp.minimum(finished, turn), 0, n_batches - 1)

    def within(u):
        return jnp.logical_and(u >= 0, u < units)

    def step(i, carry):
        for g in range(1, 5):

            @pl.when(i == gather_at[g])
            def _(g=g):
                gathers[g - 1].wait_recv()
                gathers[g].start()

        @pl.when(i == ffn_from)
        def _():
            gathers[4].wait_recv()

        @pl.when(jnp.logical_and(i % HALVES == 0, i // HALVES + lead < chunks))
        def _():
            norm_and_send(i // HALVES + lead)

        @pl.when(mid)
        def _():
            @pl.when(i + LEAD * HALVES < units)
            def _():
                pass_on(i + LEAD * HALVES)

            @pl.when(i < units)
            def _():
                both_sections(i)

        @pl.when(jnp.logical_and(outer, within(i - late)))
        def _():
            take_back(i - late)

        @pl.when(within(i - late - LAG))
        def _():
            third(i - late - LAG)

        @pl.when(within(i - late - 2 * LAG))
        def _():
            fourth(i - late - 2 * LAG)

        @pl.when(ready(i) > ready(i - 1))
        def _():
            ffn(ready(i) - 1)

        return carry

    lax.fori_loop(0, units + 3 * LAG, step, 0)

    @pl.when(mid)
    def _():
        def relays(u, carry):
            relay(u).wait_send()
            return carry

        lax.fori_loop(0, units, relays, 0)

        def downs(u, carry):
            down(u).wait_send()
            return carry

        lax.fori_loop(units - SLOTS, units, downs, 0)

    @pl.when(outer)
    def _():
        for s in range(2):
            lend(s).wait_send()

    def lasts(u, carry):
        cores(u).wait_send()
        return carry

    lax.fori_loop(units - SLOTS, units, lasts, 0)
    for gather in gathers:
        gather.wait_send()


def finish_kernel(own, gain2_ref, wf, out_ref, res, hn, acc, copy_sem, out_sem):
    chunks, halves, blk, part = own.shape
    head = chunks - BATCH
    pieces = 4
    copies = []
    for p in range(pieces):
        low, high = head * p // pieces, head * (p + 1) // pieces
        at = pl.ds(low, high - low)
        for h in range(halves):
            copies.append(
                pltpu.make_async_copy(
                    own.at[at, h],
                    out_ref.at[at, :, pl.ds(h * part, part)],
                    copy_sem.at[p * halves + h],
                )
            )
    for copy in copies:
        copy.start()
    for j in range(BATCH):
        mixed = jnp.concatenate([own[head + j, h] for h in range(halves)], axis=1)
        at = pl.ds(j * blk, blk)
        hn[at] = rms_scale(mixed, gain2_ref[...]).astype(jnp.bfloat16)
        acc[at] = mixed.astype(jnp.float32)
    mlp(hn, wf, acc)
    res[...] = acc[...].astype(jnp.bfloat16).reshape(res.shape)
    store = pltpu.make_async_copy(res, out_ref.at[pl.ds(head, BATCH)], out_sem)
    store.start()
    for copy in copies:
        copy.wait()
    store.wait()


def relayed(
    recording, mix_gain, block_weights, section_perm, block_mask, ffn_gain, ffn_in, ffn_out
):
    time_steps, local_ch, width = recording.shape
    sections, nb, _, blk, _ = block_weights.shape[1:]
    chunks = time_steps * nb
    units = chunks * HALVES
    part = width // HALVES
    shard = ffn_in.shape[-1]
    shards = lax.axis_size("mix")
    vmem = pl.BlockSpec(memory_space=pltpu.VMEM)
    smem = pl.BlockSpec(memory_space=pltpu.SMEM)
    anywhere = pl.BlockSpec(memory_space=pl.ANY)
    far = pltpu.VMEM((units, blk, part), jnp.bfloat16)
    ring = pltpu.VMEM((SLOTS, blk, part), jnp.bfloat16)
    mixed, weights = pl.pallas_call(
        functools.partial(relay_kernel, (sections, nb)),
        out_shape=(
            pltpu.VMEM((chunks, HALVES, blk, part), jnp.bfloat16),
            pltpu.VMEM((shards, 3 * width, shard), jnp.bfloat16),
        ),
        in_specs=[anywhere, vmem, anywhere, vmem, smem, vmem, anywhere, anywhere],
        out_specs=(vmem, vmem),
        scratch_shapes=[far] * 5
        + [ring] * 2
        + [
            pltpu.VMEM((sections * nb, blk, 2 * blk), jnp.bfloat16),
            pltpu.VMEM((2 * nb, blk, 2 * blk), jnp.bfloat16),
            pltpu.VMEM(block_weights.shape, jnp.bfloat16),
            pltpu.VMEM((BATCH * blk, width), jnp.bfloat16),
            pltpu.VMEM((BATCH * blk, width), jnp.float32),
            pltpu.VMEM((STREAM, blk, width), jnp.bfloat16),
            pltpu.VMEM((STREAM, blk, part), jnp.bfloat16),
            pltpu.SemaphoreType.DMA((5, units)),
            pltpu.SemaphoreType.DMA((5, units)),
            pltpu.SemaphoreType.DMA((2,)),
            pltpu.SemaphoreType.DMA((2,)),
            pltpu.SemaphoreType.DMA((5,)),
            pltpu.SemaphoreType.DMA((5,)),
            pltpu.SemaphoreType.DMA((2,)),
            pltpu.SemaphoreType.DMA((STREAM,)),
            pltpu.SemaphoreType.DMA((STREAM,)),
            pltpu.SemaphoreType.DMA,
        ],
        compiler_params=pltpu.CompilerParams(
            collective_id=1, has_side_effects=True, vmem_limit_bytes=46 * 1024 * 1024
        ),
    )(
        recording.reshape(chunks, blk, width),
        mix_gain,
        block_weights,
        section_perm,
        block_mask,
        ffn_gain,
        ffn_in,
        ffn_out,
    )
    result = pl.pallas_call(
        finish_kernel,
        out_shape=jax.ShapeDtypeStruct((chunks, blk, width), jnp.bfloat16),
        in_specs=[vmem, vmem, vmem],
        out_specs=anywhere,
        scratch_shapes=[
            pltpu.VMEM((BATCH, blk, width), jnp.bfloat16),
            pltpu.VMEM((BATCH * blk, width), jnp.bfloat16),
            pltpu.VMEM((BATCH * blk, width), jnp.float32),
            pltpu.SemaphoreType.DMA((4 * HALVES,)),
            pltpu.SemaphoreType.DMA,
        ],
        compiler_params=pltpu.CompilerParams(vmem_limit_bytes=16 * 1024 * 1024),
    )(mixed, ffn_gain, weights)
    return result.reshape(time_steps, local_ch, width)


def on_device(recording, mix_gain, block_weights, *rest):
    sections, nb = block_weights.shape[1:3]
    chunks = recording.shape[0] * nb
    fits = (
        lax.axis_size("mix") == 16
        and lax.axis_size("groups") % 2 == 0
        and sections == 4
        and chunks % BATCH == 0
        and chunks >= 32
    )
    plan = relayed if fits else exchanged
    return plan(recording, mix_gain, block_weights, *rest)


def solution(mesh):
    in_specs = (
        P("groups", "mix", None),
        P(),
        P(None, None, "mix", None, None, None),
        P(),
        P(None, None, "mix"),
        P(),
        P(None, None, None, "mix"),
        P(None, None, "mix"),
    )
    out_specs = P("groups", "mix", None)
    return jax.shard_map(
        on_device, mesh=mesh, in_specs=in_specs, out_specs=out_specs, check_vma=False
    )
```

```python
import functools

import jax
import jax.numpy as jnp
from jax import lax
from jax.experimental import pallas as pl
from jax.experimental.pallas import tpu as pltpu
from jax.sharding import PartitionSpec as P

epsilon = 1e-05
WINDOW = 4
OFFSETS = (0, 4, 7, 9)
RING = 8
FTILE = 512


def rms_scale(values, gain):
    values = values.astype(jnp.float32)
    mean_sq = jnp.mean(values * values, axis=-1, keepdims=True)
    return values * lax.rsqrt(mean_sq + epsilon) * gain


def mixing_kernel(
    dims,
    x_ref,
    gain1_ref,
    bw_ref,
    perm_ref,
    mask_ref,
    gain2_ref,
    wl_ref,
    out_ref,
    own0,
    ring,
    far,
    wc,
    wf,
    hn,
    acc,
    send_sem,
    recv_sem,
    ag_send,
    ag_recv,
    local_sem,
    out_sem,
):
    n_dev, sections, nb, batch, first_bit, split = dims
    chunks, blk, width = x_ref.shape
    hidden_units = wf.shape[1]
    shard = wl_ref.shape[1] // split
    n_batches = chunks // batch
    bits = n_dev.bit_length() - 1
    last = sections - 1
    me = lax.axis_index("mix")
    partners = [me + (1 << b) * (1 - 2 * ((me // (1 << b)) % 2)) for b in range(bits)]

    group = lax.axis_index("groups")
    sibling = group + 1 - 2 * (group % 2)
    targets = [{"mix": partners[b]} for b in range(bits)]
    if split == 2:
        targets = targets + [{"groups": sibling}]
    piece = pl.ds(pl.multiple_of((group % split) * shard, shard), shard)
    local = pltpu.make_async_copy(
        wl_ref.at[:, piece, :], wf.at[:, pl.ds(0, shard), :], local_sem
    )
    local.start()
    route = [targets[b] for b in range(bits - 1, 0, -1)] + targets[bits:] + targets[: min(bits, 1)]
    rounds = len(route)

    barrier = pltpu.get_barrier_semaphore()
    for target in targets:
        pl.semaphore_signal(
            barrier, inc=1, device_id=target, device_id_type=pl.DeviceIdType.MESH
        )
    pl.semaphore_wait(barrier, len(targets))

    def own_at(s, k):
        return own0.at[k] if s == 0 else ring.at[s - 1, k % RING]

    def exchange(s, k):
        return pltpu.make_async_remote_copy(
            src_ref=own_at(s, k),
            dst_ref=far.at[s, k],
            send_sem=send_sem.at[s, k],
            recv_sem=recv_sem.at[s, k],
            device_id={"mix": partners[first_bit - s]},
            device_id_type=pl.DeviceIdType.MESH,
        )

    def gather_step(g):
        count = shard << g
        return pltpu.make_async_remote_copy(
            src_ref=wf.at[:, pl.ds(0, count), :],
            dst_ref=wf.at[:, pl.ds(count, count), :],
            send_sem=ag_send.at[g],
            recv_sem=ag_recv.at[g],
            device_id=route[g],
            device_id_type=pl.DeviceIdType.MESH,
        )

    def norm_and_send(k):
        own0[k] = rms_scale(x_ref[k], gain1_ref[...]).astype(jnp.bfloat16)
        exchange(0, k).start()

    def first(k, carry):
        norm_and_send(k)
        return carry

    window = min(WINDOW, chunks)
    lax.fori_loop(0, window, first, 0)
    local.wait()
    if rounds:
        gather_step(0).start()

    def fold(q, carry):
        s = q // nb
        where_to = lax.broadcasted_iota(jnp.int32, (blk, blk), 1)
        hot = (perm_ref[s] == where_to).astype(jnp.float32).astype(jnp.bfloat16)
        keep = mask_ref[q].astype(jnp.float32)
        wc[q, :, :blk] = jnp.dot(
            bw_ref[q, 0], hot, preferred_element_type=jnp.float32
        ).astype(jnp.bfloat16)
        wc[q, :, blk:] = (
            keep * jnp.dot(bw_ref[q, 1], hot, preferred_element_type=jnp.float32)
        ).astype(jnp.bfloat16)
        return carry

    lax.fori_loop(0, sections * nb, fold, 0)

    def section(s, k):
        both = jnp.concatenate([own_at(s, k)[...], far[s, k]], axis=0)
        return jnp.dot(
            wc[s * nb + k % nb], both, preferred_element_type=jnp.float32
        ).astype(jnp.bfloat16)

    def ffn(b, carry):
        rows = batch * blk
        base = pl.multiple_of(b * batch, batch)
        mixed = own0[pl.ds(base, batch)].reshape(rows, width)
        hn[...] = rms_scale(mixed, gain2_ref[...]).astype(jnp.bfloat16)
        acc[...] = mixed.astype(jnp.float32)

        def tile(f, inner):
            at = pl.ds(pl.multiple_of(f * FTILE, FTILE), FTILE)
            nt = (((1,), (1,)), ((), ()))
            gate = lax.dot_general(hn[...], wf[0, at, :], nt, preferred_element_type=jnp.float32)
            up = lax.dot_general(hn[...], wf[1, at, :], nt, preferred_element_type=jnp.float32)
            hidden = (gate / (1.0 + jnp.exp(-gate)) * up).astype(jnp.bfloat16)
            acc[...] += jnp.dot(hidden, wf[2, at, :], preferred_element_type=jnp.float32)
            return inner

        lax.fori_loop(0, hidden_units // FTILE, tile, 0)
        own0[pl.ds(base, batch)] = acc[...].astype(jnp.bfloat16).reshape(batch, blk, width)
        pltpu.make_async_copy(
            own0.at[pl.ds(base, batch)], out_ref.at[pl.ds(base, batch)], out_sem.at[b]
        ).start()
        return carry

    ffn_from = 5 * chunks // 8 + 1
    gather_at = [1 + g * (ffn_from - 1) // max(rounds, 1) for g in range(rounds)]

    def ready(i):
        done = jnp.clip((i - OFFSETS[last] + 1) // batch, 0, n_batches)
        return jnp.where(i >= ffn_from, done, 0)

    def step(i, carry):
        for g in range(1, rounds):

            @pl.when(i == gather_at[g])
            def _(g=g):
                gather_step(g - 1).wait_recv()
                gather_step(g).start()

        @pl.when(i + window < chunks)
        def _():
            norm_and_send(i + window)

        for s in range(sections):
            k = i - OFFSETS[s]

            @pl.when(jnp.logical_and(k >= 0, k < chunks))
            def _(s=s, k=k):
                exchange(s, k).wait_recv()
                result = section(s, k)
                if s < last:

                    @pl.when(k >= RING)
                    def _():
                        exchange(s + 1, k - RING).wait_send()

                    own_at(s + 1, k)[...] = result
                    exchange(s + 1, k).start()
                else:
                    exchange(0, k).wait_send()
                    own0[k] = (
                        x_ref[k].astype(jnp.float32) + result.astype(jnp.float32)
                    ).astype(jnp.bfloat16)

        if rounds:

            @pl.when(i == ffn_from)
            def _():
                gather_step(rounds - 1).wait_recv()

        lax.fori_loop(ready(i - 1), ready(i), ffn, 0)
        return carry

    lax.fori_loop(0, chunks + OFFSETS[last], step, 0)

    for s in range(1, sections):
        for k in range(max(chunks - RING, 0), chunks):
            exchange(s, k).wait_send()
    for g in range(rounds):
        gather_step(g).wait_send()
    for b in range(n_batches):
        at = pl.ds(b * batch, batch)
        pltpu.make_async_copy(own0.at[at], out_ref.at[at], out_sem.at[b]).wait()


def exchanged(
    recording, mix_gain, block_weights, section_perm, block_mask, ffn_gain, ffn_in, ffn_out
):
    time_steps, local_ch, width = recording.shape
    sections, nb, _, blk, _ = block_weights.shape[1:]
    n_dev = lax.axis_size("mix")
    chunks = time_steps * nb
    batch = 4
    while chunks % batch:
        batch //= 2
    bits = n_dev.bit_length() - 1
    total_bits = (n_dev * nb).bit_length() - 1
    first_bit = total_bits - 1 - (nb.bit_length() - 1)
    shard = ffn_in.shape[-1]
    split = 2 if lax.axis_size("groups") % 2 == 0 and shard % 32 == 0 else 1
    rounds = bits + split - 1
    local_weights = jnp.concatenate(
        [jnp.swapaxes(ffn_in[0], 1, 2), jnp.swapaxes(ffn_out, 1, 2)], axis=0
    )
    vmem = pl.BlockSpec(memory_space=pltpu.VMEM)
    anywhere = pl.BlockSpec(memory_space=pl.ANY)
    result = pl.pallas_call(
        functools.partial(mixing_kernel, (n_dev, sections, nb, batch, first_bit, split)),
        out_shape=jax.ShapeDtypeStruct((chunks, blk, width), jnp.bfloat16),
        in_specs=[vmem, vmem, vmem, vmem, pl.BlockSpec(memory_space=pltpu.SMEM), vmem, anywhere],
        out_specs=anywhere,
        scratch_shapes=[
            pltpu.VMEM((chunks, blk, width), jnp.bfloat16),
            pltpu.VMEM((sections - 1, RING, blk, width), jnp.bfloat16),
            pltpu.VMEM((sections, chunks, blk, width), jnp.bfloat16),
            pltpu.VMEM((sections * nb, blk, 2 * blk), jnp.bfloat16),
            pltpu.VMEM((3, shard * n_dev, width), jnp.bfloat16),
            pltpu.VMEM((batch * blk, width), jnp.bfloat16),
            pltpu.VMEM((batch * blk, width), jnp.float32),
            pltpu.SemaphoreType.DMA((sections, chunks)),
            pltpu.SemaphoreType.DMA((sections, chunks)),
            pltpu.SemaphoreType.DMA((rounds,)),
            pltpu.SemaphoreType.DMA((rounds,)),
            pltpu.SemaphoreType.DMA,
            pltpu.SemaphoreType.DMA((chunks // batch,)),
        ],
        compiler_params=pltpu.CompilerParams(
            collective_id=0, has_side_effects=True, vmem_limit_bytes=60 * 1024 * 1024
        ),
    )(
        recording.reshape(chunks, blk, width),
        mix_gain,
        block_weights[0].reshape(sections * nb, 2, blk, blk),
        section_perm[0][:, :, None],
        block_mask[0].reshape(sections * nb),
        ffn_gain,
        local_weights,
    )
    return result.reshape(time_steps, local_ch, width)


LEAD = 6
OUTER_LEAD = 10
HALVES = 2
SLOTS = 8
STREAM = 4
BATCH = 2
GROUPED = 4
OUTER_LAG = 2
SIDE_LAG = 2
CORE_LAG = 1


def mlp(hn, wf, acc):
    tiles = wf.shape[0] // GROUPED
    width = wf.shape[1] // 3

    def weights(f, which):
        at = pl.ds(which * width, width)
        return jnp.concatenate([wf[f * GROUPED + j, at, :] for j in range(GROUPED)], axis=1)

    def inner(f):
        gate = jnp.dot(hn[...], weights(f, 0), preferred_element_type=jnp.float32)
        up_part = jnp.dot(hn[...], weights(f, 1), preferred_element_type=jnp.float32)
        return (gate / (1.0 + jnp.exp(-gate)) * up_part).astype(jnp.bfloat16)

    hidden = inner(0)
    for f in range(tiles):
        later = inner(f + 1) if f + 1 < tiles else None
        acc[...] += lax.dot_general(
            hidden, weights(f, 2), (((1,), (1,)), ((), ())), preferred_element_type=jnp.float32
        )
        hidden = later


def relay_kernel(
    dims,
    x_ref,
    gain1_hbm,
    bw_ref,
    perm_hbm,
    mask_ref,
    gain2_hbm,
    win_ref,
    wout_ref,
    own,
    wf,
    fo,
    fc,
    fr,
    f2,
    f3,
    oring,
    vring,
    wc,
    wx,
    bw,
    gain1_ref,
    perm_ref,
    gain2_ref,
    hn,
    acc,
    xin,
    xres,
    send_sem,
    recv_sem,
    wx_send,
    wx_recv,
    ag_send,
    ag_recv,
    local_sem,
    xin_sem,
    xres_sem,
    bw_sem,
    small_sem,
):
    sections, nb = dims
    chunks, blk, width = x_ref.shape
    units = chunks * HALVES
    part = width // HALVES
    shards, wrows, _ = wf.shape
    half_rows = wrows // 2
    n_batches = chunks // BATCH
    VERTICAL, CROSS, RELAY, SIDE, CORE = range(5)

    me = lax.axis_index("mix")
    group = lax.axis_index("groups")
    shift = [(1 << b) * (1 - 2 * ((me // (1 << b)) % 2)) for b in range(4)]
    z = me // 4
    mid = jnp.logical_or(z == 1, z == 2)
    outer = jnp.logical_not(mid)
    far_z = {"mix": me + shift[3]}
    near_z = {"mix": me + shift[2]}
    cross_z = {"mix": me + shift[3] + shift[2]}
    side = {"mix": me + shift[1]}
    core = {"mix": me + shift[0]}
    sibling = {"groups": group + 1 - 2 * (group % 2)}
    half = group % 2

    def x_load(k):
        return pltpu.make_async_copy(x_ref.at[k], xin.at[k % STREAM], xin_sem.at[k % STREAM])

    def x_again(u):
        at = pl.ds(pl.multiple_of((u % HALVES) * part, part), part)
        return pltpu.make_async_copy(
            x_ref.at[u // HALVES, :, at], xres.at[u % STREAM], xres_sem.at[u % STREAM]
        )

    bw_load = pltpu.make_async_copy(bw_ref, bw, bw_sem)
    small_loads = [
        pltpu.make_async_copy(gain1_hbm, gain1_ref, small_sem.at[0]),
        pltpu.make_async_copy(perm_hbm, perm_ref, small_sem.at[1]),
        pltpu.make_async_copy(gain2_hbm, gain2_ref, small_sem.at[2]),
    ]
    d_model = width
    first_half = [
        pltpu.make_async_copy(
            win_ref.at[0, 0], wf.at[0, pl.ds(0, d_model), :], local_sem.at[0]
        ),
        pltpu.make_async_copy(
            win_ref.at[0, 1, pl.ds(0, half_rows - d_model), :],
            wf.at[0, pl.ds(d_model, half_rows - d_model), :],
            local_sem.at[1],
        ),
    ]
    second_half = [
        pltpu.make_async_copy(
            win_ref.at[0, 1, pl.ds(half_rows - d_model, 2 * d_model - half_rows), :],
            wf.at[0, pl.ds(half_rows, 2 * d_model - half_rows), :],
            local_sem.at[0],
        ),
        pltpu.make_async_copy(
            wout_ref.at[0], wf.at[0, pl.ds(2 * d_model, d_model), :], local_sem.at[1]
        ),
    ]
    barrier = pltpu.get_barrier_semaphore()
    targets = [far_z, near_z, cross_z, side, core, sibling]
    for target in targets:
        pl.semaphore_signal(
            barrier, inc=1, device_id=target, device_id_type=pl.DeviceIdType.MESH
        )

    for which, copies in enumerate((first_half, second_half)):

        @pl.when(half == which)
        def _(copies=copies):
            for copy in copies:
                copy.start()

    for load in small_loads:
        load.start()
    for k in range(STREAM):
        x_load(k).start()
    bw_load.start()
    for u in range(STREAM):
        x_again(u).start()
    pl.semaphore_wait(barrier, len(targets))

    def send(kind, u, src, dst, target):
        return pltpu.make_async_remote_copy(
            src_ref=src,
            dst_ref=dst,
            send_sem=send_sem.at[kind, u],
            recv_sem=recv_sem.at[kind, u],
            device_id=target,
            device_id_type=pl.DeviceIdType.MESH,
        )

    def own_at(u):
        return own.at[u // HALVES, u % HALVES]

    def up(u):
        return send(VERTICAL, u, own_at(u), fo.at[u], near_z)

    def down(u):
        return send(VERTICAL, u, oring.at[u % SLOTS], fo.at[u], near_z)

    def cross(u):
        return send(CROSS, u, own_at(u), fc.at[u], cross_z)

    def relay(u):
        return send(RELAY, u, fo.at[u], fr.at[u], cross_z)

    def sideways(u):
        return send(SIDE, u, own_at(u), f2.at[u], side)

    def cores(u):
        return send(CORE, u, vring.at[u % SLOTS], f3.at[u], core)

    rows = pl.ds(pl.multiple_of(half * half_rows, half_rows), half_rows)
    gathers = []
    for g, target in enumerate((far_z, near_z, side, sibling, core)):
        if g < 3:
            count = 1 << g
            src = wf.at[pl.ds(0, count), rows, :]
            dst = wf.at[pl.ds(count, count), rows, :]
        elif g == 3:
            src = dst = wf.at[pl.ds(0, shards // 2), rows, :]
        else:
            src = wf.at[pl.ds(0, shards // 2)]
            dst = wf.at[pl.ds(shards // 2, shards // 2)]
        gathers.append(
            pltpu.make_async_remote_copy(
                src_ref=src,
                dst_ref=dst,
                send_sem=ag_send.at[g],
                recv_sem=ag_recv.at[g],
                device_id=target,
                device_id_type=pl.DeviceIdType.MESH,
            )
        )

    for which, copies in enumerate((first_half, second_half)):

        @pl.when(half == which)
        def _(copies=copies):
            for copy in copies:
                copy.wait()

    gathers[0].start()

    def norm_and_send(k):
        x_load(k).wait()
        normed = rms_scale(xin[k % STREAM], gain1_ref[...]).astype(jnp.bfloat16)
        for h in range(HALVES):
            u = k * HALVES + h
            own[k, h] = normed[:, h * part : (h + 1) * part]

            @pl.when(mid)
            def _(u=u):
                cross(u).start()

            @pl.when(outer)
            def _(u=u):
                up(u).start()

        @pl.when(k + STREAM < chunks)
        def _():
            x_load(k + STREAM).start()

    def first(k, carry):
        norm_and_send(k)
        return carry

    def fold(q, carry):
        s = q // nb
        n = q % nb
        what = lax.broadcasted_iota(jnp.int32, (blk, blk), 0)
        hot = (perm_ref[0, pl.ds(s, 1), :] == what).astype(jnp.float32).astype(jnp.bfloat16)
        keep = mask_ref[0, s, n].astype(jnp.float32)
        nt = (((1,), (1,)), ((), ()))
        wc[q, :, :blk] = lax.dot_general(
            bw[0, s, n, 0], hot, nt, preferred_element_type=jnp.float32
        ).astype(jnp.bfloat16)
        wc[q, :, blk:] = (
            keep
            * lax.dot_general(bw[0, s, n, 1], hot, nt, preferred_element_type=jnp.float32)
        ).astype(jnp.bfloat16)
        return carry

    def lend(s):
        at = pl.ds(s * nb, nb)
        return pltpu.make_async_remote_copy(
            src_ref=wc.at[at],
            dst_ref=wx.at[at],
            send_sem=wx_send.at[s],
            recv_sem=wx_recv.at[s],
            device_id=near_z,
            device_id_type=pl.DeviceIdType.MESH,
        )

    for load in small_loads:
        load.wait()
    lax.fori_loop(0, LEAD, first, 0)
    bw_load.wait()
    lax.fori_loop(0, 2 * nb, fold, 0)

    @pl.when(outer)
    def _():
        for s in range(2):
            lend(s).start()

    lax.fori_loop(2 * nb, sections * nb, fold, 0)

    @pl.when(outer)
    def _():
        lax.fori_loop(LEAD, OUTER_LEAD, first, 0)

    lead = jnp.where(mid, LEAD, OUTER_LEAD)

    def pass_on(u):
        up(u).wait_recv()
        relay(u).start()

    @pl.when(mid)
    def _():
        def early(u, carry):
            pass_on(u)
            return carry

        lax.fori_loop(0, LEAD * HALVES, early, 0)
        for s in range(2):
            lend(s).wait_recv()

    def mix(weights, a, b):
        return jnp.dot(
            weights, jnp.concatenate([a, b], axis=0), preferred_element_type=jnp.float32
        ).astype(jnp.bfloat16)

    def block_of(u):
        return (u // HALVES) % nb

    def both_sections(u):
        n = block_of(u)
        cross(u).wait_recv()
        mine = own[u // HALVES, u % HALVES]
        outs = fo[u]
        relay(u).wait_recv()
        y_out = mix(wx[n], outs, fc[u])
        y_own = mix(wc[n], mine, fr[u])

        @pl.when(u >= SLOTS)
        def _():
            down(u - SLOTS).wait_send()

        oring[u % SLOTS] = mix(wx[nb + n], y_out, y_own)
        down(u).start()
        cross(u).wait_send()
        own[u // HALVES, u % HALVES] = mix(wc[nb + n], y_own, y_out)
        sideways(u).start()

    def take_back(u):
        down(u).wait_recv()
        up(u).wait_send()
        own[u // HALVES, u % HALVES] = fo[u]
        sideways(u).start()

    def third(u):
        sideways(u).wait_recv()
        result = mix(wc[2 * nb + block_of(u)], own[u // HALVES, u % HALVES], f2[u])

        @pl.when(u >= SLOTS)
        def _():
            cores(u - SLOTS).wait_send()

        vring[u % SLOTS] = result
        cores(u).start()

    def fourth(u):
        x_again(u).wait()
        cores(u).wait_recv()
        result = mix(wc[3 * nb + block_of(u)], vring[u % SLOTS], f3[u])
        sideways(u).wait_send()
        own[u // HALVES, u % HALVES] = (
            xres[u % STREAM].astype(jnp.float32) + result.astype(jnp.float32)
        ).astype(jnp.bfloat16)

        @pl.when(u + STREAM < units)
        def _():
            x_again(u + STREAM).start()

    def ffn(b):
        def get(j, carry):
            k = b * BATCH + j
            mixed = jnp.concatenate([own[k, h] for h in range(HALVES)], axis=1)
            at = pl.ds(pl.multiple_of(j * blk, blk), blk)
            hn[at] = rms_scale(mixed, gain2_ref[...]).astype(jnp.bfloat16)
            acc[at] = mixed.astype(jnp.float32)
            return carry

        lax.fori_loop(0, BATCH, get, 0)
        mlp(hn, wf, acc)
        for h in range(HALVES):
            own[pl.ds(b * BATCH, BATCH), h] = (
                acc[:, h * part : (h + 1) * part].astype(jnp.bfloat16).reshape(BATCH, blk, part)
            )

    gather_at = [0, 4 * HALVES, 8 * HALVES, 11 * HALVES, 18 * HALVES]
    ffn_from = 20 * HALVES
    late = jnp.where(mid, 0, OUTER_LAG)
    batch_units = BATCH * HALVES

    def ready(i):
        finished = (i - (late + SIDE_LAG + CORE_LAG) + 1) // batch_units
        turn = i - ffn_from + 1
        return jnp.clip(jnp.minimum(finished, turn), 0, n_batches - 1)

    def within(u):
        return jnp.logical_and(u >= 0, u < units)

    def step(i, carry):
        for g in range(1, 5):

            @pl.when(i == gather_at[g])
            def _(g=g):
                gathers[g - 1].wait_recv()
                gathers[g].start()

        @pl.when(i == ffn_from)
        def _():
            gathers[4].wait_recv()

        @pl.when(jnp.logical_and(i % HALVES == 0, i // HALVES + lead < chunks))
        def _():
            norm_and_send(i // HALVES + lead)

        @pl.when(mid)
        def _():
            @pl.when(i + LEAD * HALVES < units)
            def _():
                pass_on(i + LEAD * HALVES)

            @pl.when(i < units)
            def _():
                both_sections(i)

        @pl.when(jnp.logical_and(outer, within(i - late)))
        def _():
            take_back(i - late)

        @pl.when(within(i - late - SIDE_LAG))
        def _():
            third(i - late - SIDE_LAG)

        @pl.when(within(i - late - SIDE_LAG - CORE_LAG))
        def _():
            fourth(i - late - SIDE_LAG - CORE_LAG)

        @pl.when(ready(i) > ready(i - 1))
        def _():
            ffn(ready(i) - 1)

        return carry

    lax.fori_loop(0, units + OUTER_LAG + SIDE_LAG + CORE_LAG, step, 0)

    @pl.when(mid)
    def _():
        def relays(u, carry):
            relay(u).wait_send()
            return carry

        lax.fori_loop(0, units, relays, 0)

        def downs(u, carry):
            down(u).wait_send()
            return carry

        lax.fori_loop(units - SLOTS, units, downs, 0)

    @pl.when(outer)
    def _():
        for s in range(2):
            lend(s).wait_send()

    def lasts(u, carry):
        cores(u).wait_send()
        return carry

    lax.fori_loop(units - SLOTS, units, lasts, 0)
    for gather in gathers:
        gather.wait_send()


def finish_kernel(own, gain2_ref, wf, out_ref, res, hn, acc, copy_sem, out_sem):
    chunks, halves, blk, part = own.shape
    head = chunks - BATCH
    pieces = 4
    copies = []
    for p in range(pieces):
        low, high = head * p // pieces, head * (p + 1) // pieces
        at = pl.ds(low, high - low)
        for h in range(halves):
            copies.append(
                pltpu.make_async_copy(
                    own.at[at, h],
                    out_ref.at[at, :, pl.ds(h * part, part)],
                    copy_sem.at[p * halves + h],
                )
            )
    for copy in copies:
        copy.start()
    for j in range(BATCH):
        mixed = jnp.concatenate([own[head + j, h] for h in range(halves)], axis=1)
        at = pl.ds(j * blk, blk)
        hn[at] = rms_scale(mixed, gain2_ref[...]).astype(jnp.bfloat16)
        acc[at] = mixed.astype(jnp.float32)
    mlp(hn, wf, acc)
    res[...] = acc[...].astype(jnp.bfloat16).reshape(res.shape)
    store = pltpu.make_async_copy(res, out_ref.at[pl.ds(head, BATCH)], out_sem)
    store.start()
    for copy in copies:
        copy.wait()
    store.wait()


def relayed(
    recording, mix_gain, block_weights, section_perm, block_mask, ffn_gain, ffn_in, ffn_out
):
    time_steps, local_ch, width = recording.shape
    sections, nb, _, blk, _ = block_weights.shape[1:]
    chunks = time_steps * nb
    units = chunks * HALVES
    part = width // HALVES
    shard = ffn_in.shape[-1]
    shards = lax.axis_size("mix")
    vmem = pl.BlockSpec(memory_space=pltpu.VMEM)
    smem = pl.BlockSpec(memory_space=pltpu.SMEM)
    anywhere = pl.BlockSpec(memory_space=pl.ANY)
    far = pltpu.VMEM((units, blk, part), jnp.bfloat16)
    ring = pltpu.VMEM((SLOTS, blk, part), jnp.bfloat16)
    mixed, weights = pl.pallas_call(
        functools.partial(relay_kernel, (sections, nb)),
        out_shape=(
            pltpu.VMEM((chunks, HALVES, blk, part), jnp.bfloat16),
            pltpu.VMEM((shards, 3 * width, shard), jnp.bfloat16),
        ),
        in_specs=[anywhere] * 4 + [smem] + [anywhere] * 3,
        out_specs=(vmem, vmem),
        scratch_shapes=[far] * 5
        + [ring] * 2
        + [
            pltpu.VMEM((sections * nb, blk, 2 * blk), jnp.bfloat16),
            pltpu.VMEM((2 * nb, blk, 2 * blk), jnp.bfloat16),
            pltpu.VMEM(block_weights.shape, jnp.bfloat16),
            pltpu.VMEM(mix_gain.shape, jnp.float32),
            pltpu.VMEM(section_perm.shape, jnp.int32),
            pltpu.VMEM(ffn_gain.shape, jnp.float32),
            pltpu.VMEM((BATCH * blk, width), jnp.bfloat16),
            pltpu.VMEM((BATCH * blk, width), jnp.float32),
            pltpu.VMEM((STREAM, blk, width), jnp.bfloat16),
            pltpu.VMEM((STREAM, blk, part), jnp.bfloat16),
            pltpu.SemaphoreType.DMA((5, units)),
            pltpu.SemaphoreType.DMA((5, units)),
            pltpu.SemaphoreType.DMA((2,)),
            pltpu.SemaphoreType.DMA((2,)),
            pltpu.SemaphoreType.DMA((5,)),
            pltpu.SemaphoreType.DMA((5,)),
            pltpu.SemaphoreType.DMA((2,)),
            pltpu.SemaphoreType.DMA((STREAM,)),
            pltpu.SemaphoreType.DMA((STREAM,)),
            pltpu.SemaphoreType.DMA,
            pltpu.SemaphoreType.DMA((3,)),
        ],
        compiler_params=pltpu.CompilerParams(
            collective_id=1, has_side_effects=True, vmem_limit_bytes=46 * 1024 * 1024
        ),
    )(
        recording.reshape(chunks, blk, width),
        mix_gain,
        block_weights,
        section_perm,
        block_mask,
        ffn_gain,
        ffn_in,
        ffn_out,
    )
    result = pl.pallas_call(
        finish_kernel,
        out_shape=jax.ShapeDtypeStruct((chunks, blk, width), jnp.bfloat16),
        in_specs=[vmem, vmem, vmem],
        out_specs=anywhere,
        scratch_shapes=[
            pltpu.VMEM((BATCH, blk, width), jnp.bfloat16),
            pltpu.VMEM((BATCH * blk, width), jnp.bfloat16),
            pltpu.VMEM((BATCH * blk, width), jnp.float32),
            pltpu.SemaphoreType.DMA((4 * HALVES,)),
            pltpu.SemaphoreType.DMA,
        ],
        compiler_params=pltpu.CompilerParams(vmem_limit_bytes=16 * 1024 * 1024),
    )(mixed, ffn_gain, weights)
    return result.reshape(time_steps, local_ch, width)


def on_device(recording, mix_gain, block_weights, *rest):
    sections, nb = block_weights.shape[1:3]
    chunks = recording.shape[0] * nb
    fits = (
        lax.axis_size("mix") == 16
        and lax.axis_size("groups") % 2 == 0
        and sections == 4
        and chunks % BATCH == 0
        and chunks >= 32
    )
    plan = relayed if fits else exchanged
    return plan(recording, mix_gain, block_weights, *rest)


def solution(mesh):
    in_specs = (
        P("groups", "mix", None),
        P(),
        P(None, None, "mix", None, None, None),
        P(),
        P(None, None, "mix"),
        P(),
        P(None, None, None, "mix"),
        P(None, None, "mix"),
    )
    out_specs = P("groups", "mix", None)
    return jax.shard_map(
        on_device, mesh=mesh, in_specs=in_specs, out_specs=out_specs, check_vma=False
    )
```
